32 devices in a mesh: fsdp: 16 (over z, y, core), seq: 2 (over x).
Axes of the slice: x: 2, y: 2, z: 4, core: 2. Of those that a mesh axis runs over, the one named last changes fastest.
Arguments:
- tokens_in: bfloat16 [16, 512, 768], P('fsdp', 'seq'), may hold values from -6 to 6
- patches: bfloat16 [16, 2048, 768], P('fsdp', 'seq'), may hold values from -6 to 6
- segment_ids: int32 [16, 512], P('fsdp'), may hold values from 0 to 15, never falling along the last dimension, each value on 1 to 64 neighbouring positions
- key_valid: int32 [16, 512], P('fsdp'), may hold values 0 or 1
- out_grad: bfloat16 [16, 512, 768], P('fsdp', 'seq'), may hold values from -6 to 6
- self_gain: bfloat16 [768], P('fsdp'), may hold values from 0.5 to 1.5
- self_query: bfloat16 [768, 768], P('fsdp'), may hold values from -0.21875 to 0.21875
- self_key: bfloat16 [768, 768], P('fsdp'), may hold values from -0.21875 to 0.21875
- self_value: bfloat16 [768, 768], P('fsdp'), may hold values from -0.21875 to 0.21875
- self_output: bfloat16 [768, 768], P('fsdp'), may hold values from -0.875 to 0.875
- cross_gain: bfloat16 [768], P('fsdp'), may hold values from 0.5 to 1.5
- cross_query: bfloat16 [768, 768], P('fsdp'), may hold values from -0.21875 to 0.21875
- cross_key: bfloat16 [768, 768], P('fsdp'), may hold values from -0.21875 to 0.21875
- cross_value: bfloat16 [768, 768], P('fsdp'), may hold values from -0.21875 to 0.21875
- cross_output: bfloat16 [768, 768], P('fsdp'), may hold values from -2.5 to 2.5
- mlp_gain: bfloat16 [768], P('fsdp'), may hold values from 0.5 to 1.5
- mlp_gate: bfloat16 [768, 2048], P('fsdp'), may hold values from -0.21875 to 0.21875
- mlp_up: bfloat16 [768, 2048], P('fsdp'), may hold values from -0.21875 to 0.21875
- mlp_down: bfloat16 [2048, 768], P('fsdp'), may hold values from -0.125 to 0.125
Outputs:
- layer_out: bfloat16 [16, 512, 768], P('fsdp', 'seq')
- input_grad: float32 [16, 512, 768], P('fsdp', 'seq')
- patch_grad: float32 [16, 2048, 768], P('fsdp', 'seq')
- self_gain_grad: float32 [768], P('fsdp')
- self_query_grad: float32 [768, 768], P('fsdp')
- self_key_grad: float32 [768, 768], P('fsdp')
- self_value_grad: float32 [768, 768], P('fsdp')
- self_output_grad: float32 [768, 768], P('fsdp')
- cross_gain_grad: float32 [768], P('fsdp')
- cross_query_grad: float32 [768, 768], P('fsdp')
- cross_key_grad: float32 [768, 768], P('fsdp')
- cross_value_grad: float32 [768, 768], P('fsdp')
- cross_output_grad: float32 [768, 768], P('fsdp')
- mlp_gain_grad: float32 [768], P('fsdp')
- mlp_gate_grad: float32 [768, 2048], P('fsdp')
- mlp_up_grad: float32 [768, 2048], P('fsdp')
- mlp_down_grad: float32 [2048, 768], P('fsdp')
The draws below stay inside these ranges and needn't reach their ends.
Inputs may be any that keep to these rules, and one draw needn't show every extreme that they name: `segment_ids`: along an item's row the answer number never falls; every answer has 1 to 64 tokens.
All inputs are finite; a program needn't handle non-finite values. No bound on the sum of `key_valid` on one device may be relied on, other than what follows from the above.
Results may differ from the reference program's by a relative error of at most 0.023.
Values may be sent and summed in bfloat16 or wider, within the bound.
No kernel may reach another device: no remote copies, remote signals or barrier semaphores. Data moves between devices by JAX's collectives and lax.ppermute only.
A program may use at most 192 MiB of HBM per device.

```python
import math
import jax
import jax.numpy as jnp
import numpy as np
from jax import lax

D = 768
H = 12
DH = 64
FF = 2048
HD = 768
TOK = 512
PATCH = 2048
SEGS = 16
ITEMS = 16


def place_ends(values, rng, low, top_value):
    extent = values.shape
    spot = [jax.random.randint(jax.random.fold_in(rng, axis), (), 0, extent[axis]) for axis in range(len(extent))]
    values = values.at[tuple(spot)].set(low)
    longest = extent.index(max(extent))
    spot[longest] = (spot[longest] + 1) % extent[longest]
    return values.at[tuple(spot)].set(top_value)


def strengthened(drawn, stream_key, source, target, blocks, factor):
    def block_of(axis_at):
        return (jnp.arange(drawn.shape[axis_at]) // (drawn.shape[axis_at] // blocks)).reshape((-1,) + (1,) * (drawn.ndim - 1 - axis_at))

    near = jax.random.permutation(stream_key, blocks)[block_of(target)]
    second = (block_of(target) + blocks // 2) % blocks
    return jnp.where((block_of(source) == near) | (block_of(source) == second), factor * drawn, drawn)


def level_of(key, extent, pieces, low, top_value):
    factor_of = 1.0
    for dim, blocks in pieces:
        steps = jax.random.uniform(jax.random.fold_in(jax.random.fold_in(key, 6), dim), (blocks,), jnp.float32, low / len(pieces), top_value / len(pieces))
        factor_of = factor_of * jnp.repeat(jnp.exp(steps), extent[dim] // blocks).reshape((-1,) + (1,) * (len(extent) - 1 - dim))
    return factor_of


def split_up(count, total, most, skew):
    loads = [(1 << 20) // math.isqrt(standing ** skew) + 1 for standing in range(2, count + 1)]
    rest, given = total - most - (count - 1), [1] * (count - 1)
    while rest > 0:
        free = [i for i in range(count - 1) if given[i] < most]
        mass, left = sum([loads[i] for i in free]), rest
        for i in free:
            addition = min(most - given[i], max(1, left * loads[i] // mass), rest)
            given[i] = given[i] + addition
            rest = rest - addition
    return np.array([most] + given)


def uneven(stream_key, count, total, most, slope):
    if count == 2:
        one = jax.random.randint(stream_key, (), max(1, total - most), min(most, total - 1) + 1)
        return jnp.stack([one, total - one])
    tallies = jnp.asarray(split_up(count, total, most, slope), jnp.int32)
    twos = (count - 1) // 2
    source_of, taker = tallies[1:1 + 2 * twos:2], tallies[2:2 + 2 * twos:2]
    slack = jnp.minimum(source_of - 1, most - taker)
    passed = jax.random.randint(jax.random.fold_in(stream_key, 1), (twos,), 0, 1 << 20) % (slack + 1)
    tallies = tallies.at[1:1 + 2 * twos:2].set(source_of - passed).at[2:2 + 2 * twos:2].set(taker + passed)
    return tallies[jax.random.permutation(jax.random.fold_in(stream_key, 2), count)]


def normal_values(key, shape, scale, reach, split=(), kind=jnp.bfloat16):
    result = jax.random.normal(key, shape, jnp.float32) * scale
    if len(split) > 0:
        result = level_of(key, shape, split, -0.22, 0.18) * result
    return jnp.clip(result, min=-reach, max=reach).astype(kind)


def bell_draw_with(stream_key, extent, spread, bound, cuts, heavy, kind=jnp.bfloat16):
    values = spread * jax.random.normal(stream_key, extent, jnp.float32)
    if cuts:
        values = values * level_of(stream_key, extent, cuts, -0.22, 0.18)
    return jnp.clip(strengthened(values, jax.random.fold_in(stream_key, 3), *heavy), -bound, bound).astype(kind)


def setup_inputs(seed: int = 0) -> dict:
    streams_of = jax.random.split(jax.random.key(seed), 20)
    return {
        "tokens_in": bell_draw_with(streams_of[0], (ITEMS, TOK, D), 1.0, 6.0, ((0, 16), (1, 2)), (0, 2, 16, 2.0)),
        "patches": bell_draw_with(streams_of[1], (ITEMS, PATCH, D), 1.0, 6.0, ((0, 16), (1, 2)), (0, 2, 16, 2.0)),
        "segment_ids": jax.vmap(lambda own: jnp.searchsorted(jnp.cumsum(uneven(own, SEGS, TOK, TOK // 8, 2)), jnp.arange(TOK), side="right"))(jax.random.split(streams_of[2], ITEMS)).reshape((ITEMS, TOK)).astype(jnp.int32),
        "key_valid": place_ends((jax.random.randint(streams_of[3], (ITEMS, TOK), 0, 8) < 7).astype(jnp.int32), jax.random.fold_in(streams_of[3], 1), 0, 1),
        "out_grad": normal_values(streams_of[4], (ITEMS, TOK, D), 1.0, 6.0, ((0, 16), (1, 2))),
        "self_gain": jnp.clip(1.0 + 0.1 * jax.random.normal(streams_of[5], (D,), jnp.float32), 0.5, 1.5).astype(jnp.bfloat16),
        "self_query": normal_values(streams_of[6], (D, HD), D ** -0.5, 0.21875, ((0, 16),)),
        "self_key": normal_values(streams_of[7], (D, HD), D ** -0.5, 0.21875, ((0, 16),)),
        "self_value": normal_values(streams_of[8], (D, HD), D ** -0.5, 0.21875, ((0, 16),)),
        "self_output": normal_values(streams_of[9], (HD, D), (max(HD // 16, 1)) ** -0.5, 0.875, ((0, 16),)),
        "cross_gain": jnp.clip(1.0 + 0.1 * jax.random.normal(streams_of[10], (D,), jnp.float32), 0.5, 1.5).astype(jnp.bfloat16),
        "cross_query": normal_values(streams_of[11], (D, HD), D ** -0.5, 0.21875, ((0, 16),)),
        "cross_key": normal_values(streams_of[12], (D, HD), D ** -0.5, 0.21875, ((0, 16),)),
        "cross_value": normal_values(streams_of[13], (D, HD), D ** -0.5, 0.21875, ((0, 16),)),
        "cross_output": normal_values(streams_of[14], (HD, D), (max(HD // 128, 1)) ** -0.5, 2.5, ((0, 16),)),
        "mlp_gain": jnp.clip(1.0 + 0.1 * jax.random.normal(streams_of[15], (D,), jnp.float32), 0.5, 1.5).astype(jnp.bfloat16),
        "mlp_gate": normal_values(streams_of[16], (D, FF), D ** -0.5, 0.21875, ((0, 16),)),
        "mlp_up": normal_values(streams_of[17], (D, FF), D ** -0.5, 0.21875, ((0, 16),)),
        "mlp_down": normal_values(streams_of[18], (FF, D), FF ** -0.5, 0.125, ((0, 16),)),
    }


EPSILON = 1e-06
SCORE_SCALE = 0.125
MASKED = -1e+30

@jax.custom_vjp
def low(v):
    return lax.optimization_barrier(v.astype(jnp.bfloat16)).astype(jnp.float32)

@jax.custom_vjp
def low_back(v):
    return v

def low_keep(v):
    return (low(v), None)

def low_pass(kept, grad):
    return (grad,)

def back_keep(v):
    return (v, None)

def back_low(kept, grad):
    return (low(grad),)
low.defvjp(low_keep, low_pass)
low_back.defvjp(back_keep, back_low)

def round_both(tensor):
    return low(low_back(tensor))

def product(factor_left, factor_right):
    return jnp.dot(factor_left, factor_right, precision=lax.Precision.HIGHEST)

def rms_norm(tensor, scale_vec):
    return tensor * lax.rsqrt(lax.optimization_barrier(jnp.mean(tensor * tensor, axis=-1, keepdims=True)) + EPSILON) * scale_vec

def attend(query_rows, keys_all, values_all, allowed):
    heads_q = query_rows.reshape(query_rows.shape[0], H, DH)
    heads_k = keys_all.reshape(keys_all.shape[0], H, DH)
    heads_v = values_all.reshape(values_all.shape[0], H, DH)
    scores = low_back(SCORE_SCALE * jnp.einsum('qhd,khd->hqk', heads_q, heads_k, precision=lax.Precision.HIGHEST))
    if allowed is not None:
        scores = jnp.where(allowed[None], scores, MASKED)
    weights = low(jax.nn.softmax(scores, axis=-1))
    mixed_heads = jnp.einsum('hqk,khd->qhd', weights, heads_v, precision=lax.Precision.HIGHEST)
    return round_both(mixed_heads.reshape(query_rows.shape[0], HD))

def layer_item(params, member):
    gain_one, query_w, key_w, value_w, output_w, gain_two, cquery_w, ckey_w, cvalue_w, coutput_w, gain_three, gate_w, up_w, down_w = params
    tokens, patch_rows, segments, valid_keys = member
    position = jnp.arange(TOK, dtype=jnp.int32)
    earlier = position[None, :] <= position[:, None]
    own_key = position[None, :] == position[:, None]
    allowed = (segments[:, None] == segments[None, :]) & earlier & ((valid_keys[None, :] == 1) | own_key)
    normed = low(rms_norm(tokens, gain_one))
    mixed_one = attend(round_both(product(normed, query_w)), round_both(product(normed, key_w)), round_both(product(normed, value_w)), allowed)
    hidden_one = tokens + low_back(product(mixed_one, output_w))
    normed = low(rms_norm(hidden_one, gain_two))
    mixed_two = attend(round_both(product(normed, cquery_w)), round_both(product(patch_rows, ckey_w)), round_both(product(patch_rows, cvalue_w)), None)
    hidden_two = hidden_one + low_back(product(mixed_two, coutput_w))
    normed = low(rms_norm(hidden_two, gain_three))
    gate_pre = low_back(product(normed, gate_w))
    up_pre = low_back(product(normed, up_w))
    inner_act = low(jax.nn.gelu(gate_pre, approximate=True) * up_pre)
    return hidden_two + low_back(product(inner_act, down_w))

def reference(tokens_in, patches, segment_ids, key_valid, out_grad, self_gain, self_query, self_key, self_value, self_output, cross_gain, cross_query, cross_key, cross_value, cross_output, mlp_gain, mlp_gate, mlp_up, mlp_down):
    weight_list = tuple((weight.astype(jnp.float32) for weight in (self_gain, self_query, self_key, self_value, self_output, cross_gain, cross_query, cross_key, cross_value, cross_output, mlp_gain, mlp_gate, mlp_up, mlp_down)))

    def forward_pass(tokens, patch_rows, params):
        checked = jax.checkpoint(layer_item)
        return lax.map(lambda member: checked(params, member), (tokens, patch_rows, segment_ids, key_valid))
    layer_out, pullback = jax.vjp(forward_pass, tokens_in.astype(jnp.float32), patches.astype(jnp.float32), weight_list)
    input_grad, patch_grad, grads = pullback(out_grad.astype(jnp.float32))
    return (layer_out.astype(jnp.bfloat16), input_grad, patch_grad, grads[0], grads[1], grads[2], grads[3], grads[4], grads[5], grads[6], grads[7], grads[8], grads[9], grads[10], grads[11], grads[12], grads[13])
```

```python
import jax
import jax.numpy as jnp
from jax import lax
from jax.sharding import PartitionSpec as P

DH = 64
EPSILON = 1e-06
SCORE_SCALE = 0.125
MASKED = -1e30
BF = jnp.bfloat16
F4 = jnp.float32


def mm(a, b):
    return jnp.dot(a, b, preferred_element_type=F4)


def mm_nt(a, b):
    return lax.dot_general(a, b, (((1,), (1,)), ((), ())), preferred_element_type=F4)


def mm_tn(a, b):
    return lax.dot_general(a, b, (((0,), (0,)), ((), ())), preferred_element_type=F4)


def swap(value):
    return lax.ppermute(value, "seq", [(0, 1), (1, 0)])


def inv_rms(value):
    return lax.rsqrt(jnp.mean(value * value, axis=-1, keepdims=True) + EPSILON)


def norm_back(value, inv, gain, grad):
    unit = value * inv
    scaled = grad * gain
    dot = jnp.mean(scaled * unit, axis=-1, keepdims=True)
    return (scaled - unit * dot) * inv, jnp.sum(grad * unit, axis=0, keepdims=True)


def heads_of(value):
    return value.reshape(value.shape[0], -1, DH).transpose(1, 0, 2)


def rows_of(value):
    return value.transpose(1, 0, 2).reshape(value.shape[1], -1)


def attend_forward(query, key, value, allowed):
    def one_head(operands):
        q, k, v = operands
        scores = SCORE_SCALE * mm_nt(q, k)
        if allowed is not None:
            scores = jnp.where(allowed, scores, MASKED)
        highest = jnp.max(scores, axis=-1, keepdims=True)
        total = highest + jnp.log(jnp.sum(jnp.exp(scores - highest), axis=-1, keepdims=True))
        weights = jnp.exp(scores - total).astype(BF)
        return mm(weights, v).astype(BF), total

    mixed, totals = lax.map(one_head, (heads_of(query), heads_of(key), heads_of(value)))
    return rows_of(mixed), totals


def attend_backward(query, key, value, allowed, totals, grad):
    def one_head(operands):
        q, k, v, total, g = operands
        scores = SCORE_SCALE * mm_nt(q, k)
        if allowed is not None:
            scores = jnp.where(allowed, scores, MASKED)
        weights = jnp.exp(scores - total)
        dp = mm_nt(g, v)
        carried = jnp.sum(weights * dp, axis=-1, keepdims=True)
        ds = (weights * (dp - carried)).astype(BF)
        dq = (SCORE_SCALE * mm(ds, k)).astype(BF)
        dk = (SCORE_SCALE * mm_tn(ds, q)).astype(BF)
        dv = mm_tn(weights.astype(BF), g).astype(BF)
        return dq, dk, dv

    dq, dk, dv = lax.map(
        one_head, (heads_of(query), heads_of(key), heads_of(value), totals, heads_of(grad))
    )
    return rows_of(dq), rows_of(dk), rows_of(dv)


def gelu_parts(z):
    c = 0.7978845608028654
    t = jnp.tanh(c * (z + 0.044715 * z * z * z))
    act = 0.5 * z * (1.0 + t)
    slope = 0.5 * (1.0 + t) + 0.5 * z * (1.0 - t * t) * (c * (1.0 + 3.0 * 0.044715 * z * z))
    return act, slope


def local(
    tokens_in,
    patches,
    segment_ids,
    key_valid,
    out_grad,
    self_gain,
    self_query,
    self_key,
    self_value,
    self_output,
    cross_gain,
    cross_query,
    cross_key,
    cross_value,
    cross_output,
    mlp_gain,
    mlp_gate,
    mlp_up,
    mlp_down,
):
    side = lax.axis_index("seq")
    first = side == 0
    fsdp = lax.axis_size("fsdp")
    tok_half, width = tokens_in.shape[1:]
    patch_half = patches.shape[1]
    tok_total = segment_ids.shape[1]
    hidden = self_query.shape[1]
    half = hidden // 2
    ff_half = mlp_gate.shape[1] // 2
    ff_own = ff_half // fsdp
    own_row = side * tok_half
    own_col = side * half

    def ordered(mine, other, axis):
        return jnp.concatenate(
            [jnp.where(first, mine, other), jnp.where(first, other, mine)], axis=axis
        )

    def own_cols(weight):
        return lax.dynamic_slice_in_dim(weight, own_col, half, 1)

    def ff_cols(weight):
        split = weight.reshape(weight.shape[0], fsdp, 2, ff_own)
        mine = jnp.where(first, split[:, :, 0], split[:, :, 1])
        return mine.reshape(weight.shape[0], ff_half)

    gains = jnp.stack([self_gain, cross_gain, mlp_gain], axis=1)
    gains = jnp.pad(gains, ((0, 0), (0, 125)))
    cq_pair = jnp.concatenate(
        [
            jnp.where(first, cross_query[:, :half], cross_query[:, half:]),
            jnp.where(first, cross_query[:, half:], cross_query[:, :half]),
        ],
        axis=1,
    )
    shard = jnp.concatenate(
        [
            own_cols(self_query),
            own_cols(self_key),
            own_cols(self_value),
            gains,
            own_cols(cross_key),
            own_cols(cross_value),
            self_output,
            cq_pair,
            cross_output,
            ff_cols(mlp_gate),
            ff_cols(mlp_up),
        ],
        axis=1,
    )
    whole = lax.all_gather(shard, "fsdp", axis=0, tiled=True)
    w_down = lax.all_gather(
        lax.dynamic_slice_in_dim(mlp_down, side * ff_own, ff_own, 0), "fsdp", axis=0, tiled=True
    )
    at = 0
    pieces = []
    for size in (3 * half, 128, 2 * half, hidden, hidden, hidden, 2 * ff_half):
        pieces.append(whole[:, at : at + size])
        at += size
    w_qkv, gain_cols, w_ckv, w_so, w_cq, w_co, w_gu = pieces
    gain_rows = gain_cols.T.astype(F4)
    gain_one, gain_two, gain_three = gain_rows[0:1], gain_rows[1:2], gain_rows[2:3]

    tok_other = swap(tokens_in[0])
    grad_other = swap(out_grad[0])
    patch_other = swap(patches[0])
    x = ordered(tokens_in[0], tok_other, 0).astype(F4)
    g3 = ordered(out_grad[0], grad_other, 0)
    m = jnp.concatenate([patches[0], patch_other], axis=0)

    pos = jnp.arange(tok_total, dtype=jnp.int32)
    seg = segment_ids[0]
    valid = key_valid[0]
    allowed = (
        (seg[:, None] == seg[None, :])
        & (pos[None, :] <= pos[:, None])
        & ((valid[None, :] == 1) | (pos[None, :] == pos[:, None]))
    )

    inv_one = inv_rms(x)
    n1 = (x * inv_one * gain_one).astype(BF)
    qkv = mm(n1, w_qkv).astype(BF)
    q1, k1, v1 = qkv[:, :half], qkv[:, half : 2 * half], qkv[:, 2 * half :]
    o_own, lse_one = attend_forward(q1, k1, v1, allowed)
    o_all = ordered(o_own, swap(o_own), 1)
    h1 = x + mm(o_all, w_so)

    ckv = mm(m, w_ckv).astype(BF)
    kc, vc = ckv[:, :half], ckv[:, half:]
    inv_two = inv_rms(h1)
    n2 = (h1 * inv_two * gain_two).astype(BF)
    qc = mm(n2, w_cq[:, :half]).astype(BF)
    oc_own, lse_two = attend_forward(qc, kc, vc, None)
    oc_all = ordered(oc_own, swap(oc_own), 1)
    h2 = h1 + mm(oc_all, w_co)

    inv_three = inv_rms(h2)
    n3 = (h2 * inv_three * gain_three).astype(BF)
    ab = mm(n3, w_gu)
    act, slope = gelu_parts(ab[:, :ff_half])
    b = ab[:, ff_half:]
    u = (act * b).astype(BF)
    y = mm(u, w_down)

    def own_rows(value):
        return lax.dynamic_slice_in_dim(value, own_row, tok_half, 0)

    def other_rows(value):
        return lax.dynamic_slice_in_dim(value, tok_half - own_row, tok_half, 0)

    layer_out = (own_rows(h2) + own_rows(y) + swap(other_rows(y).astype(BF)).astype(F4)).astype(BF)

    du = mm_nt(g3, w_down)
    dab = jnp.concatenate([(du * b * slope).astype(BF), (du * act).astype(BF)], axis=1)
    dn3 = mm_nt(dab, w_gu)
    dn3 = dn3 + swap(dn3.astype(BF)).astype(F4)
    grad_gu = lax.psum_scatter(
        mm_tn(n3, dab).astype(BF), "fsdp", scatter_dimension=0, tiled=True
    )
    grad_down = lax.psum_scatter(mm_tn(u, g3).astype(BF), "fsdp", scatter_dimension=0, tiled=True)
    dh, gg3 = norm_back(h2, inv_three, gain_three, dn3)
    d1 = g3.astype(F4) + dh
    d1b = d1.astype(BF)

    grad_co = mm_tn(oc_all, own_cols(d1b)).astype(BF)
    doc = mm_nt(d1b, lax.dynamic_slice_in_dim(w_co, own_col, half, 0)).astype(BF)
    dqc, dkc, dvc = attend_backward(qc, kc, vc, None, lse_two, doc)
    dqc_pair = jnp.concatenate([dqc, swap(dqc)], axis=1)
    dh, gg2 = norm_back(h1, inv_two, gain_two, mm_nt(dqc_pair, w_cq))
    d2 = d1 + dh
    d2b = d2.astype(BF)
    dckv = jnp.concatenate([dkc, dvc], axis=1)
    part_other = mm_nt(dckv[patch_half:], w_ckv).astype(BF)
    patch_grad = mm_nt(dckv[:patch_half], w_ckv) + swap(part_other).astype(F4)
    grad_cq = mm_tn(n2, dqc).astype(BF)
    grad_ckv = mm_tn(m, dckv).astype(BF)

    grad_so = mm_tn(o_all, own_cols(d2b)).astype(BF)
    do = mm_nt(d2b, lax.dynamic_slice_in_dim(w_so, own_col, half, 0)).astype(BF)
    dqkv = jnp.concatenate(attend_backward(q1, k1, v1, allowed, lse_one, do), axis=1)
    grad_qkv = mm_tn(n1, dqkv).astype(BF)
    dn1 = mm_nt(dqkv, w_qkv)
    dn1 = own_rows(dn1) + swap(other_rows(dn1).astype(BF)).astype(F4)
    dx, gg1 = norm_back(own_rows(x), own_rows(inv_one), gain_one, dn1)
    input_grad = own_rows(d2) + dx

    gain_grads = jnp.concatenate([gg1, gg2, gg3, jnp.zeros((125, width), F4)], axis=0)
    packed = jnp.concatenate(
        [grad_co, grad_cq, grad_ckv, grad_so, grad_qkv, gain_grads.T.astype(BF)], axis=1
    )
    share = lax.psum_scatter(packed, "fsdp", scatter_dimension=0, tiled=True)

    share_other = swap(share)
    gu_other = swap(grad_gu)
    down_other = swap(grad_down)

    def pair(at):
        return ordered(share[:, at : at + half], share_other[:, at : at + half], 1).astype(F4)

    def ff_pair(at):
        mine = grad_gu[:, at : at + ff_half].reshape(-1, fsdp, 1, ff_own)
        other = gu_other[:, at : at + ff_half].reshape(-1, fsdp, 1, ff_own)
        return ordered(mine, other, 2).reshape(-1, 2 * ff_half).astype(F4)

    g_at = 8 * half
    mine = share[:, g_at : g_at + 3].astype(F4)
    other = share_other[:, g_at : g_at + 3].astype(F4)
    return (
        layer_out[None],
        input_grad[None],
        patch_grad[None],
        mine[:, 0] + other[:, 0],
        pair(5 * half),
        pair(6 * half),
        pair(7 * half),
        pair(4 * half),
        mine[:, 1],
        pair(half),
        pair(2 * half),
        pair(3 * half),
        pair(0),
        mine[:, 2],
        ff_pair(0),
        ff_pair(ff_half),
        ordered(grad_down, down_other, 0).astype(F4),
    )


def solution(mesh):
    rows = P("fsdp", None)
    items = P("fsdp", "seq", None)
    vec = P("fsdp")
    in_specs = (
        (items, items, rows, rows, items)
        + (vec, rows, rows, rows, rows) * 2
        + (vec, rows, rows, rows)
    )
    out_specs = (
        (items, items, items)
        + (vec, rows, rows, rows, rows) * 2
        + (vec, rows, rows, rows)
    )
    return jax.shard_map(local, mesh=mesh, in_specs=in_specs, out_specs=out_specs, check_vma=False)
```

```python
import functools

import jax
import jax.numpy as jnp
from jax import lax
from jax.experimental import pallas as pl
from jax.experimental.pallas import tpu as pltpu
from jax.sharding import PartitionSpec as P

DH = 64
EPSILON = 1e-06
SCORE_SCALE = 0.125
MASKED = -1e30
BF = jnp.bfloat16
F4 = jnp.float32


def mm(a, b):
    return jnp.dot(a, b, preferred_element_type=F4)


def mm_nt(a, b):
    return lax.dot_general(a, b, (((1,), (1,)), ((), ())), preferred_element_type=F4)


def mm_tn(a, b):
    return lax.dot_general(a, b, (((0,), (0,)), ((), ())), preferred_element_type=F4)


def swap(value):
    return lax.ppermute(value, "seq", [(0, 1), (1, 0)])


def inv_rms(value):
    return lax.rsqrt(jnp.mean(value * value, axis=-1, keepdims=True) + EPSILON)


def norm_back(value, inv, gain, grad):
    unit = value * inv
    scaled = grad * gain
    dot = jnp.mean(scaled * unit, axis=-1, keepdims=True)
    return (scaled - unit * dot) * inv, jnp.sum(grad * unit, axis=0, keepdims=True)


def lanes_of_head():
    odd = lax.rem(pl.program_id(0), 2)
    lane = lax.broadcasted_iota(jnp.int32, (1, 2 * DH), 1)
    return odd, (lane >= DH) == (odd == 1)


def keep_lanes(ref, at, value, odd, mine):
    value = value.astype(ref.dtype)

    @pl.when(odd == 0)
    def _():
        ref[at] = value

    @pl.when(odd == 1)
    def _():
        ref[at] = jnp.where(mine, value, ref[at])


def fold_rows(value):
    return value.reshape(value.shape[0] // 8, 8, value.shape[1])


def forward_kernel(masked, chunk, q_ref, k_ref, v_ref, *rest):
    bias_ref = rest[0] if masked else None
    o_ref, inv_ref, e_ref, s_ref, acc_ref = rest[-5:]
    odd, mine = lanes_of_head()
    count = k_ref.shape[0] // chunk
    q = jnp.where(mine, q_ref[...].astype(F4) * SCORE_SCALE, 0.0).astype(BF)
    top = jnp.full((8, q.shape[0]), -jnp.inf, F4)
    for c in range(count):
        rows = pl.ds(c * chunk, chunk)
        scores = mm_nt(k_ref[rows, :], q)
        if masked:
            scores = scores + bias_ref[rows, :]
        s_ref[rows, :] = scores
        top = jnp.maximum(top, jnp.max(fold_rows(scores), axis=0))
    top = jnp.max(top, axis=0, keepdims=True)
    total = jnp.zeros((8, q.shape[0]), F4)
    for c in range(count):
        rows = pl.ds(c * chunk, chunk)
        e = jnp.exp(s_ref[rows, :] - top)
        total = total + jnp.sum(fold_rows(e), axis=0)
        e = e.astype(BF)
        e_ref[0, rows, :] = e
        part = mm_tn(v_ref[rows, :], e)
        acc_ref[...] = part if c == 0 else acc_ref[...] + part
    inv = 1.0 / jnp.sum(total, axis=0, keepdims=True)
    whole = (slice(None), slice(None))
    keep_lanes(o_ref, whole, (acc_ref[...] * inv).T, odd, mine)
    keep_lanes(inv_ref, whole, jnp.broadcast_to(inv, acc_ref.shape).T, odd, mine)


def attend_forward(query, key, value, bias):
    rows, width = query.shape
    keys = key.shape[0]
    heads = width // DH
    chunk = min(keys, 512)

    def pair(size):
        return pl.BlockSpec((size, 2 * DH), lambda h: (0, h // 2))

    specs = [pair(rows), pair(keys), pair(keys)]
    args = [query, key, value]
    if bias is not None:
        specs.append(pl.BlockSpec((keys, rows), lambda h: (0, 0)))
        args.append(bias)
    return pl.pallas_call(
        functools.partial(forward_kernel, bias is not None, chunk),
        grid=(heads,),
        in_specs=specs,
        out_specs=[pair(rows), pair(rows), pl.BlockSpec((1, keys, rows), lambda h: (h, 0, 0))],
        out_shape=[
            jax.ShapeDtypeStruct((rows, width), BF),
            jax.ShapeDtypeStruct((rows, width), F4),
            jax.ShapeDtypeStruct((heads, keys, rows), BF),
        ],
        scratch_shapes=[pltpu.VMEM((keys, rows), F4), pltpu.VMEM((2 * DH, rows), F4)],
        compiler_params=pltpu.CompilerParams(vmem_limit_bytes=40 << 20),
        cost_estimate=pl.CostEstimate(
            flops=4 * heads * rows * keys * 256,
            bytes_accessed=2 * heads * rows * keys,
            transcendentals=heads * rows * keys,
        ),
        name="attend_forward",
    )(*args)


def backward_kernel(chunk, e_ref, q_ref, k_ref, v_ref, g_ref, o_ref, dq_ref, dk_ref, dv_ref, acc_ref):
    odd, mine = lanes_of_head()
    count = k_ref.shape[0] // chunk
    q = (q_ref[...].astype(F4) * SCORE_SCALE).astype(BF)
    g = g_ref[...]
    own = jnp.where(mine, g.astype(F4), 0.0)
    carried = jnp.sum((own * o_ref[...].astype(F4)).T, axis=0, keepdims=True)
    own = own.astype(BF)
    for c in range(count):
        rows = pl.ds(c * chunk, chunk)
        e = e_ref[0, rows, :]
        dp = mm_nt(v_ref[rows, :], own)
        ds = (e.astype(F4) * (dp - carried)).astype(BF)
        at = (rows, slice(None))
        keep_lanes(dv_ref, at, mm(e, g), odd, mine)
        keep_lanes(dk_ref, at, mm(ds, q), odd, mine)
        part = mm_tn(k_ref[rows, :], ds)
        acc_ref[...] = part if c == 0 else acc_ref[...] + part
    keep_lanes(dq_ref, (slice(None), slice(None)), acc_ref[...].T * SCORE_SCALE, odd, mine)


def attend_backward(query, key, value, mixed, inv, weights, grad):
    rows, width = query.shape
    keys = key.shape[0]
    heads = width // DH
    chunk = min(keys, 512)
    grad = (grad.astype(F4) * inv).astype(BF)

    def pair(size):
        return pl.BlockSpec((size, 2 * DH), lambda h: (0, h // 2))

    return pl.pallas_call(
        functools.partial(backward_kernel, chunk),
        grid=(heads,),
        in_specs=[
            pl.BlockSpec((1, keys, rows), lambda h: (h, 0, 0)),
            pair(rows),
            pair(keys),
            pair(keys),
            pair(rows),
            pair(rows),
        ],
        out_specs=[pair(rows), pair(keys), pair(keys)],
        out_shape=[
            jax.ShapeDtypeStruct((rows, width), BF),
            jax.ShapeDtypeStruct((keys, width), BF),
            jax.ShapeDtypeStruct((keys, width), BF),
        ],
        scratch_shapes=[pltpu.VMEM((2 * DH, rows), F4)],
        compiler_params=pltpu.CompilerParams(vmem_limit_bytes=40 << 20),
        cost_estimate=pl.CostEstimate(
            flops=8 * heads * rows * keys * 256,
            bytes_accessed=2 * heads * rows * keys,
            transcendentals=0,
        ),
        name="attend_backward",
    )(weights, query, key, value, grad, mixed)


def gelu_parts(z):
    c = 0.7978845608028654
    t = jnp.tanh(c * (z + 0.044715 * z * z * z))
    act = 0.5 * z * (1.0 + t)
    slope = 0.5 * (1.0 + t) + 0.5 * z * (1.0 - t * t) * (c * (1.0 + 3.0 * 0.044715 * z * z))
    return act, slope


def local(
    tokens_in,
    patches,
    segment_ids,
    key_valid,
    out_grad,
    self_gain,
    self_query,
    self_key,
    self_value,
    self_output,
    cross_gain,
    cross_query,
    cross_key,
    cross_value,
    cross_output,
    mlp_gain,
    mlp_gate,
    mlp_up,
    mlp_down,
):
    side = lax.axis_index("seq")
    first = side == 0
    fsdp = lax.axis_size("fsdp")
    tok_half, width = tokens_in.shape[1:]
    patch_half = patches.shape[1]
    tok_total = segment_ids.shape[1]
    hidden = self_query.shape[1]
    half = hidden // 2
    ff_half = mlp_gate.shape[1] // 2
    ff_own = ff_half // fsdp
    own_row = side * tok_half
    own_col = side * half

    def ordered(mine, other, axis):
        return jnp.concatenate(
            [jnp.where(first, mine, other), jnp.where(first, other, mine)], axis=axis
        )

    def own_cols(weight):
        return lax.dynamic_slice_in_dim(weight, own_col, half, 1)

    def ff_cols(weight):
        split = weight.reshape(weight.shape[0], fsdp, 2, ff_own)
        mine = jnp.where(first, split[:, :, 0], split[:, :, 1])
        return mine.reshape(weight.shape[0], ff_half)

    gains = jnp.stack([self_gain, cross_gain, mlp_gain], axis=1)
    gains = jnp.pad(gains, ((0, 0), (0, 125)))
    cq_pair = jnp.concatenate(
        [
            jnp.where(first, cross_query[:, :half], cross_query[:, half:]),
            jnp.where(first, cross_query[:, half:], cross_query[:, :half]),
        ],
        axis=1,
    )
    shard = jnp.concatenate(
        [
            own_cols(self_query),
            own_cols(self_key),
            own_cols(self_value),
            gains,
            own_cols(cross_key),
            own_cols(cross_value),
            self_output,
            cq_pair,
            cross_output,
            ff_cols(mlp_gate),
            ff_cols(mlp_up),
        ],
        axis=1,
    )
    whole = lax.all_gather(shard, "fsdp", axis=0, tiled=True)
    w_down = lax.all_gather(
        lax.dynamic_slice_in_dim(mlp_down, side * ff_own, ff_own, 0), "fsdp", axis=0, tiled=True
    )
    at = 0
    pieces = []
    for size in (3 * half, 128, 2 * half, hidden, hidden, hidden, 2 * ff_half):
        pieces.append(whole[:, at : at + size])
        at += size
    w_qkv, gain_cols, w_ckv, w_so, w_cq, w_co, w_gu = pieces
    gain_rows = gain_cols.T.astype(F4)
    gain_one, gain_two, gain_three = gain_rows[0:1], gain_rows[1:2], gain_rows[2:3]

    tok_other = swap(tokens_in[0])
    grad_other = swap(out_grad[0])
    patch_other = swap(patches[0])
    x = ordered(tokens_in[0], tok_other, 0).astype(F4)
    g3 = ordered(out_grad[0], grad_other, 0)
    m = jnp.concatenate([patches[0], patch_other], axis=0)

    pos = jnp.arange(tok_total, dtype=jnp.int32)
    seg = segment_ids[0]
    valid = key_valid[0]
    allowed = (
        (seg[:, None] == seg[None, :])
        & (pos[:, None] <= pos[None, :])
        & ((valid[:, None] == 1) | (pos[:, None] == pos[None, :]))
    )
    bias = jnp.where(allowed, 0.0, MASKED).astype(F4)

    inv_one = inv_rms(x)
    n1 = (x * inv_one * gain_one).astype(BF)
    qkv = mm(n1, w_qkv).astype(BF)
    q1, k1, v1 = qkv[:, :half], qkv[:, half : 2 * half], qkv[:, 2 * half :]
    o_own, inv_l1, e1 = attend_forward(q1, k1, v1, bias)
    o_all = ordered(o_own, swap(o_own), 1)
    h1 = x + mm(o_all, w_so)

    ckv = mm(m, w_ckv).astype(BF)
    kc, vc = ckv[:, :half], ckv[:, half:]
    inv_two = inv_rms(h1)
    n2 = (h1 * inv_two * gain_two).astype(BF)
    qc = mm(n2, w_cq[:, :half]).astype(BF)
    oc_own, inv_l2, e2 = attend_forward(qc, kc, vc, None)
    oc_all = ordered(oc_own, swap(oc_own), 1)
    h2 = h1 + mm(oc_all, w_co)

    inv_three = inv_rms(h2)
    n3 = (h2 * inv_three * gain_three).astype(BF)
    ab = mm(n3, w_gu)
    act, slope = gelu_parts(ab[:, :ff_half])
    b = ab[:, ff_half:]
    u = (act * b).astype(BF)
    y = mm(u, w_down)

    def own_rows(value):
        return lax.dynamic_slice_in_dim(value, own_row, tok_half, 0)

    def other_rows(value):
        return lax.dynamic_slice_in_dim(value, tok_half - own_row, tok_half, 0)

    layer_out = (own_rows(h2) + own_rows(y) + swap(other_rows(y).astype(BF)).astype(F4)).astype(BF)

    du = mm_nt(g3, w_down)
    dab = jnp.concatenate([(du * b * slope).astype(BF), (du * act).astype(BF)], axis=1)
    dn3 = mm_nt(dab, w_gu)
    dn3 = dn3 + swap(dn3.astype(BF)).astype(F4)
    grad_gu = lax.psum_scatter(
        mm_tn(n3, dab).astype(BF), "fsdp", scatter_dimension=0, tiled=True
    )
    grad_down = lax.psum_scatter(mm_tn(u, g3).astype(BF), "fsdp", scatter_dimension=0, tiled=True)
    dh, gg3 = norm_back(h2, inv_three, gain_three, dn3)
    d1 = g3.astype(F4) + dh
    d1b = d1.astype(BF)

    grad_co = mm_tn(oc_all, own_cols(d1b)).astype(BF)
    doc = mm_nt(d1b, lax.dynamic_slice_in_dim(w_co, own_col, half, 0)).astype(BF)
    dqc, dkc, dvc = attend_backward(qc, kc, vc, oc_own, inv_l2, e2, doc)
    dqc_pair = jnp.concatenate([dqc, swap(dqc)], axis=1)
    dh, gg2 = norm_back(h1, inv_two, gain_two, mm_nt(dqc_pair, w_cq))
    d2 = d1 + dh
    d2b = d2.astype(BF)
    dckv = jnp.concatenate([dkc, dvc], axis=1)
    part_other = mm_nt(dckv[patch_half:], w_ckv).astype(BF)
    patch_grad = mm_nt(dckv[:patch_half], w_ckv) + swap(part_other).astype(F4)
    grad_cq = mm_tn(n2, dqc).astype(BF)
    grad_ckv = mm_tn(m, dckv).astype(BF)

    grad_so = mm_tn(o_all, own_cols(d2b)).astype(BF)
    do = mm_nt(d2b, lax.dynamic_slice_in_dim(w_so, own_col, half, 0)).astype(BF)
    dqkv = jnp.concatenate(attend_backward(q1, k1, v1, o_own, inv_l1, e1, do), axis=1)
    grad_qkv = mm_tn(n1, dqkv).astype(BF)
    dn1 = mm_nt(dqkv, w_qkv)
    dn1 = own_rows(dn1) + swap(other_rows(dn1).astype(BF)).astype(F4)
    dx, gg1 = norm_back(own_rows(x), own_rows(inv_one), gain_one, dn1)
    input_grad = own_rows(d2) + dx

    gain_grads = jnp.concatenate([gg1, gg2, gg3, jnp.zeros((125, width), F4)], axis=0)
    packed = jnp.concatenate(
        [grad_co, grad_cq, grad_ckv, grad_so, grad_qkv, gain_grads.T.astype(BF)], axis=1
    )
    share = lax.psum_scatter(packed, "fsdp", scatter_dimension=0, tiled=True)

    share_other = swap(share)
    gu_other = swap(grad_gu)
    down_other = swap(grad_down)

    def pair(at):
        return ordered(share[:, at : at + half], share_other[:, at : at + half], 1).astype(F4)

    def ff_pair(at):
        mine = grad_gu[:, at : at + ff_half].reshape(-1, fsdp, 1, ff_own)
        other = gu_other[:, at : at + ff_half].reshape(-1, fsdp, 1, ff_own)
        return ordered(mine, other, 2).reshape(-1, 2 * ff_half).astype(F4)

    g_at = 8 * half
    mine = share[:, g_at : g_at + 3].astype(F4)
    other = share_other[:, g_at : g_at + 3].astype(F4)
    return (
        layer_out[None],
        input_grad[None],
        patch_grad[None],
        mine[:, 0] + other[:, 0],
        pair(5 * half),
        pair(6 * half),
        pair(7 * half),
        pair(4 * half),
        mine[:, 1],
        pair(half),
        pair(2 * half),
        pair(3 * half),
        pair(0),
        mine[:, 2],
        ff_pair(0),
        ff_pair(ff_half),
        ordered(grad_down, down_other, 0).astype(F4),
    )


def solution(mesh):
    rows = P("fsdp", None)
    items = P("fsdp", "seq", None)
    vec = P("fsdp")
    in_specs = (
        (items, items, rows, rows, items)
        + (vec, rows, rows, rows, rows) * 2
        + (vec, rows, rows, rows)
    )
    out_specs = (
        (items, items, items)
        + (vec, rows, rows, rows, rows) * 2
        + (vec, rows, rows, rows)
    )
    return jax.shard_map(local, mesh=mesh, in_specs=in_specs, out_specs=out_specs, check_vma=False)
```
